128 devices in a mesh: prow: 8 (over y, core), pcol: 16 (over x, z).
Axes of the slice: x: 4, y: 4, z: 4, core: 2. Of those that a mesh axis runs over, the one named last changes fastest.
Arguments:
- diag_block: float32 [512, 512], P(('prow', 'pcol')), as said below
- panel: float32 [4, 4096, 512], P(None, ('prow', 'pcol')), may hold values from -2.4 to 2.4
- trailing: float32 [4, 4096, 2, 8192], P(None, 'prow', None, 'pcol'), may hold values from -6 to 6
Outputs:
- factor_diag: float32 [512, 512], P(('prow', 'pcol'))
- factor_panel: float32 [4, 4096, 512], P(None, ('prow', 'pcol'))
- updated: float32 [4, 4096, 2, 8192], P(None, 'prow', None, 'pcol')
The draws below stay inside these ranges and needn't reach their ends.
Inputs may be any that keep to these rules, and one draw needn't show every extreme that they name: diag_block is symmetric positive definite with eigenvalues of at least 1.
All inputs are finite; a program needn't handle non-finite values.
Results may differ from the reference program's by a relative error of at most 0.0003.
Values sent between devices are 32-bit elements; how exact they have to be, the bound alone decides.
A program may use at most 128 MiB of HBM per device.

```python
import jax
import jax.numpy as jnp
from jax import lax

B = 512
RBLK = 32
N_PROW = 8
N_PCOL = 16


def draw_diag_block(key, part):
    inner = jax.random.fold_in(key, 7)
    matrix = jax.random.normal(inner, (B, B), jnp.float32)
    matrix = matrix / jnp.sqrt(jnp.float32(B))
    return jnp.dot(matrix, matrix.T, precision=lax.Precision.HIGHEST) + jnp.eye(B, dtype=jnp.float32)


def levels(key, extent, pieces, low, largest):
    factor_of, own = 1.0, jax.random.fold_in(key, 6)
    for position, shards_of in pieces:
        heights = jnp.exp(jax.random.uniform(jax.random.fold_in(own, position), (shards_of,), jnp.float32, low / len(pieces), largest / len(pieces)))
        factor_of = factor_of * jnp.repeat(heights, extent[position] // shards_of).reshape([-1 if axis == position else 1 for axis in range(len(extent))])
    return factor_of


def centred(rng, shape, scale, bound, split=(), kind=jnp.bfloat16):
    result = jax.random.normal(rng, shape, jnp.float32) * scale
    if len(split) > 0:
        result = levels(rng, shape, split, -0.22, 0.18) * result
    return jnp.clip(result, min=-bound, max=bound).astype(kind)


def setup_inputs(seed: int = 0) -> dict:
    key_list = jax.random.split(jax.random.key(seed), 4)
    return {
        "diag_block": draw_diag_block(jax.random.fold_in(key_list[3], 71), 0),
        "panel": centred(key_list[1], (RBLK // N_PROW, N_PROW * B, B), 0.3, 2.4, ((1, 128),), jnp.float32),
        "trailing": centred(key_list[2], (RBLK // N_PROW, N_PROW * B, RBLK // N_PCOL, N_PCOL * B), 1.0, 6.0, ((1, 8), (3, 16)), jnp.float32),
    }


def reference(diag_block, panel, trailing):
    lower = jnp.linalg.cholesky(diag_block)
    rows = panel.reshape(-1, B)
    solved = jax.scipy.linalg.solve_triangular(lower, rows.T, lower=True).T
    blocks = solved.reshape(RBLK, B, B)
    whole = trailing.reshape(RBLK, B, RBLK, B)
    columns = jnp.arange(RBLK, dtype=jnp.int32)

    def one_row(index):
        left = lax.dynamic_index_in_dim(blocks, index, 0, keepdims=False)
        block_row = lax.dynamic_index_in_dim(whole, index, 0, keepdims=False)
        present = (columns <= index).astype(jnp.float32)
        product = jnp.einsum('ik,sjk->isj', left, blocks, precision=lax.Precision.HIGHEST)
        return block_row - present[None, :, None] * product
    updated = lax.map(one_row, jnp.arange(RBLK, dtype=jnp.int32))
    return (lower, solved.reshape(panel.shape), updated.reshape(trailing.shape))
```

```python
import functools

import jax
import jax.numpy as jnp
from jax import lax
from jax.experimental import pallas as pl
from jax.experimental.pallas import tpu as pltpu
from jax.sharding import Mesh
from jax.sharding import PartitionSpec as P

PROW = ("prow_0", "prow_1")
PCOL = ("pcol_0", "pcol_1")
PROW_PCOL = ("prow_0", "prow_1", "pcol_0", "pcol_1")


def in_order(blocks, dim):
    blocks = jnp.moveaxis(blocks, 0, dim)
    dims = blocks.shape
    return blocks.reshape(*dims[:dim], dims[dim] * dims[dim + 1], *dims[dim + 2 :])


def stacked_from(value, axes, turns):
    blocks = value
    for k in turns:
        blocks = lax.all_gather(blocks, axes[k])
    done = turns[::-1]
    back = [done.index(k) for k in range(len(axes))]
    blocks = blocks.transpose(*back, *range(len(axes), blocks.ndim))
    return blocks.reshape(-1, *value.shape)


def gather_axes(value, axes, turns, dim):
    return in_order(stacked_from(value, axes, turns), dim)


def padded_to(lines, peers):
    spare = -lines.shape[0] % peers
    if not spare:
        return lines
    return jnp.concatenate([lines, jnp.zeros((spare, *lines.shape[1:]), lines.dtype)])


def spread(value, axis, root):
    lines = jnp.where(lax.axis_index(axis) == root, value, jnp.zeros_like(value)).reshape(
        -1, *value.shape[1:][-1:]
    )
    padded = padded_to(lines, lax.axis_size(axis))
    own = lax.psum_scatter(padded, axis, scatter_dimension=0, tiled=True)
    return lax.all_gather(own, axis, axis=0, tiled=True)[: len(lines)].reshape(value.shape)


HI = lax.Precision.HIGHEST
F32 = jnp.float32

def tdot(a, b, prec=HI):
    return lax.dot_general(a, b, (((0,), (0,)), ((), ())), precision=prec, preferred_element_type=F32)

def bc(col, n=128):
    return jnp.broadcast_to(col, (col.shape[0], n))

def elim8(G, c0, sub):
    n = len(G)
    C = [[bc(G[g][:, c0 + j:c0 + j + 1]) for j in range(8)] for g in range(n)]
    L = [G[g][:, :128] for g in range(n)]
    V = [G[g][:, 128:] for g in range(n)]
    dv = None
    for j in range(8):
        piv = [jnp.broadcast_to(C[0][l][j:j + 1, :], (8, 128)) for l in range(j, 8)]
        rinv = 1.0 / piv[0]
        rowL = jnp.broadcast_to(L[0][j:j + 1, :], (8, 128))
        rowV = jnp.broadcast_to(V[0][j:j + 1, :], (8, 128))
        dv = piv[0] if j == 0 else jnp.where(sub == j, piv[0], dv)
        for g in range(n):
            m = C[g][j] * rinv
            if g == 0:
                m = jnp.where(sub > j, m, 0.0)
            for l in range(j + 1, 8):
                C[g][l] = C[g][l] - m * piv[l - j]
            L[g] = L[g] - m * rowL
            V[g] = V[g] - m * rowV
    sc = lax.rsqrt(dv)
    L[0] = L[0] * sc
    V[0] = V[0] * sc
    return [jnp.concatenate([L[g], V[g]], 1) for g in range(n)]

def leaf(T):
    sub = lax.broadcasted_iota(jnp.int32, (8, 128), 0)
    for sb in range(4):
        r0 = 32 * sb
        G = [T[r0 + 8 * g:r0 + 8 * g + 8, :] for g in range(4)]
        done = []
        for g in range(4):
            G = elim8(G, r0 + 8 * g, sub)
            done.append(G[0])
            T[r0 + 8 * g:r0 + 8 * g + 8, :] = G[0]
            G = G[1:]
        if sb < 3:
            W = jnp.concatenate(done, 0)
            Pm = tdot(W[:, :128], W)
            T[r0 + 32:128, :] = T[r0 + 32:128, :] - Pm[r0 + 32:128, :]

def chol_body(M, T, U, nb=4):
    row = lax.broadcasted_iota(jnp.int32, (128, 128), 0)
    col = lax.broadcasted_iota(jnp.int32, (128, 128), 1)
    eye = jnp.where(row == col, 1.0, 0.0).astype(F32)
    n = nb * 128
    for k in range(nb):
        a, b = k * 128, (k + 1) * 128
        T[:, :128] = M[a:b, a:b]
        T[:, 128:] = eye
        leaf(T)
        Ukk = jnp.where(col >= row, T[:, :128], 0.0)
        Vkk = jnp.where(col <= row, T[:, 128:], 0.0)
        U[a:b, a:b] = Ukk
        if k > 0:
            U[a:b, :a] = jnp.zeros((128, a), F32)
            M[a:b, :a] = jnp.dot(Vkk, M[a:b, :a], precision=HI, preferred_element_type=F32)
        M[a:b, a:b] = Vkk
        if k < nb - 1:
            Ur = jnp.dot(Vkk, M[a:b, b:], precision=HI, preferred_element_type=F32)
            U[a:b, b:] = Ur
            M[a:b, b:] = jnp.zeros((128, n - b), F32)
            if k > 0:
                M[b:, :a] = M[b:, :a] - tdot(Ur, M[a:b, :a])
            M[b:, a:b] = -tdot(Ur, Vkk)
            M[b:, b:] = M[b:, b:] - tdot(Ur, Ur)
F32 = jnp.float32
BF16 = jnp.bfloat16

def halves(x):
    hi = x.astype(BF16)
    return hi, (x - hi.astype(F32)).astype(BF16)

def left3(x):
    hi, lo = halves(x)
    return jnp.concatenate([hi, hi, lo], 1)

def right3(x):
    hi, lo = halves(x)
    return jnp.concatenate([hi, lo, hi], 1)

def ndot(a, b):
    return lax.dot_general(a, b, (((1,), (1,)), ((), ())), preferred_element_type=F32)

def solve_rows(x, l0, l1):
    return jnp.concatenate([ndot(left3(x[:, :256]), l0), ndot(left3(x), l1)], 1)

def update_kernel(p_of, q_of, inv, xcol, xrow, c, fpan, out, l0, l1, cols, fs):
    step = pl.program_id(0)
    p, q = p_of(), q_of()
    u, h = step // 2, step % 2

    @pl.when(step == 0)
    def _():
        l0[...] = right3(inv[:256, :256])
        l1[...] = right3(inv[256:, :])
        for k in range(4):
            cols[256 * k:256 * (k + 1), :] = right3(solve_rows(xcol[256 * k:256 * (k + 1), :], l0[...], l1[...]))

    f = solve_rows(xrow[...], l0[...], l1[...])
    fs[...] = f

    @pl.when(q // 8 == h)
    def _():
        fpan[0] = fs[pl.ds(pl.multiple_of((q % 8) * 32, 32), 32), :]

    f3 = left3(f)
    for v in range(2):
        present = v * 16 + q <= u * 8 + p

        @pl.when(present)
        def _():
            prod = ndot(f3, cols[512 * v:512 * (v + 1), :])
            for t in range(4):
                at = pl.ds(2 * t + v, 256, stride=8)
                out[at, :] = c[at, :] - prod[:, 128 * t:128 * (t + 1)]

        @pl.when(jnp.logical_not(present))
        def _():
            for t in range(4):
                at = pl.ds(2 * t + v, 256, stride=8)
                out[at, :] = c[at, :]

def update(p_of, q_of, inv, xcol, xrow, c):
    whole = lambda s: (0, 0)
    return pl.pallas_call(
        functools.partial(update_kernel, p_of, q_of),
        grid=(8,),
        in_specs=[
            pl.BlockSpec((512, 512), whole),
            pl.BlockSpec((1024, 512), whole),
            pl.BlockSpec((256, 512), lambda s: (s, 0)),
            pl.BlockSpec((2048, 128), lambda s: (s, 0)),
        ],
        out_specs=[
            pl.BlockSpec((1, 32, 512), lambda s: (s // 2, 0, 0)),
            pl.BlockSpec((2048, 128), lambda s: (s, 0)),
        ],
        out_shape=[jax.ShapeDtypeStruct((4, 32, 512), F32), jax.ShapeDtypeStruct((16384, 128), F32)],
        scratch_shapes=[pltpu.VMEM((256, 768), BF16), pltpu.VMEM((256, 1536), BF16),
                        pltpu.VMEM((1024, 1536), BF16), pltpu.VMEM((256, 512), F32)],
        compiler_params=pltpu.CompilerParams(vmem_limit_bytes=50 << 20),
        name="panel_update",
    )(inv, xcol, xrow, c)


def factor_kernel(a_ref, inv_ref, upper_ref, M, T):
    M[...] = a_ref[...]
    chol_body(M, T, upper_ref)
    inv_ref[...] = M[...]


def factor(a):
    return pl.pallas_call(
        factor_kernel,
        out_shape=[jax.ShapeDtypeStruct((512, 512), F32)] * 2,
        scratch_shapes=[pltpu.VMEM((512, 512), F32), pltpu.VMEM((128, 256), F32)],
        name="factor",
        cost_estimate=pl.CostEstimate(flops=10**10, bytes_accessed=3 << 20, transcendentals=0),
    )(a)


def per_device(diag_block, panel, trailing):
    p, q = lax.axis_index(PROW), lax.axis_index(PCOL)
    whole_diag = gather_axes(diag_block, PROW_PCOL, (0, 2, 3, 1), 0)
    row_blocks = lax.all_gather(panel, PCOL, axis=1, tiled=True)
    grouped = row_blocks.reshape(2, 2, 512, 512)
    chosen = lax.dynamic_index_in_dim(grouped, q // 8, 1, keepdims=False)
    col_blocks = spread(chosen, PROW, q % 8)
    inv, upper = factor(whole_diag)
    factor_diag = lax.dynamic_slice(upper, (0, (p * 16 + q) * 4), (512, 4)).T
    c = trailing.reshape(4, 512, 2, 4, 128).transpose(0, 1, 3, 2, 4).reshape(16384, 128)
    factor_panel, out = update(
        lambda: lax.axis_index(PROW), lambda: lax.axis_index(PCOL),
        inv, col_blocks.reshape(1024, 512), row_blocks.reshape(2048, 512), c,
    )
    updated = out.reshape(4, 512, 4, 2, 128).transpose(0, 1, 3, 2, 4).reshape(4, 512, 2, 512)
    return factor_diag, factor_panel, updated


def solution(mesh):
    finer = Mesh(mesh.devices.reshape(4, 2, 4, 4), ("prow_0", "prow_1", "pcol_0", "pcol_1"))
    specs = (P(PROW_PCOL, None), P(None, PROW_PCOL, None), P(None, PROW, None, PCOL))
    return jax.shard_map(per_device, mesh=finer, in_specs=specs, out_specs=specs, check_vma=False)
```

```python
import functools

import jax
import jax.numpy as jnp
from jax import lax
from jax.experimental import pallas as pl
from jax.experimental.pallas import tpu as pltpu
from jax.sharding import PartitionSpec as P

F32 = jnp.float32
BF16 = jnp.bfloat16
HI = lax.Precision.HIGHEST
MESH = pl.DeviceIdType.MESH


def tdot(a, b, prec=HI):
    return lax.dot_general(a, b, (((0,), (0,)), ((), ())), precision=prec, preferred_element_type=F32)

def bc(col, n=128):
    return jnp.broadcast_to(col, (col.shape[0], n))

def elim8(G, c0, sub):
    n = len(G)
    C = [[bc(G[g][:, c0 + j:c0 + j + 1]) for j in range(8)] for g in range(n)]
    L = [G[g][:, :128] for g in range(n)]
    V = [G[g][:, 128:] for g in range(n)]
    dv = None
    for j in range(8):
        piv = [jnp.broadcast_to(C[0][l][j:j + 1, :], (8, 128)) for l in range(j, 8)]
        rinv = 1.0 / piv[0]
        rowL = jnp.broadcast_to(L[0][j:j + 1, :], (8, 128))
        rowV = jnp.broadcast_to(V[0][j:j + 1, :], (8, 128))
        dv = piv[0] if j == 0 else jnp.where(sub == j, piv[0], dv)
        for g in range(n):
            m = C[g][j] * rinv
            if g == 0:
                m = jnp.where(sub > j, m, 0.0)
            for l in range(j + 1, 8):
                C[g][l] = C[g][l] - m * piv[l - j]
            L[g] = L[g] - m * rowL
            V[g] = V[g] - m * rowV
    sc = lax.rsqrt(dv)
    L[0] = L[0] * sc
    V[0] = V[0] * sc
    return [jnp.concatenate([L[g], V[g]], 1) for g in range(n)]

def leaf(T, hook, k):
    sub = lax.broadcasted_iota(jnp.int32, (8, 128), 0)
    for sb in range(4):
        r0 = 32 * sb
        G = [T[r0 + 8 * g:r0 + 8 * g + 8, :] for g in range(4)]
        done = []
        for g in range(4):
            G = elim8(G, r0 + 8 * g, sub)
            done.append(G[0])
            T[r0 + 8 * g:r0 + 8 * g + 8, :] = G[0]
            G = G[1:]
        hook(4 * k + sb)
        if sb < 3:
            W = jnp.concatenate(done, 0)
            Pm = tdot(W[:, :128], W)
            T[r0 + 32:128, :] = T[r0 + 32:128, :] - Pm[r0 + 32:128, :]

def chol_body(M, T, U, hook, nb=4):
    row = lax.broadcasted_iota(jnp.int32, (128, 128), 0)
    col = lax.broadcasted_iota(jnp.int32, (128, 128), 1)
    eye = jnp.where(row == col, 1.0, 0.0).astype(F32)
    n = nb * 128
    for k in range(nb):
        a, b = k * 128, (k + 1) * 128
        T[:, :128] = M[a:b, a:b]
        T[:, 128:] = eye
        leaf(T, hook, k)
        Ukk = jnp.where(col >= row, T[:, :128], 0.0)
        Vkk = jnp.where(col <= row, T[:, 128:], 0.0)
        U[a:b, a:b] = Ukk
        if k > 0:
            U[a:b, :a] = jnp.zeros((128, a), F32)
            M[a:b, :a] = jnp.dot(Vkk, M[a:b, :a], precision=HI, preferred_element_type=F32)
        M[a:b, a:b] = Vkk
        if k < nb - 1:
            Ur = jnp.dot(Vkk, M[a:b, b:], precision=HI, preferred_element_type=F32)
            U[a:b, b:] = Ur
            M[a:b, b:] = jnp.zeros((128, n - b), F32)
            if k > 0:
                M[b:, :a] = M[b:, :a] - tdot(Ur, M[a:b, :a])
            M[b:, a:b] = -tdot(Ur, Vkk)
            M[b:, b:] = M[b:, b:] - tdot(Ur, Ur)


def halves(x):
    hi = x.astype(BF16)
    return hi, (x - hi.astype(F32)).astype(BF16)


def left3(x):
    hi, lo = halves(x)
    return jnp.concatenate([hi, hi, lo], 1)


def right3(x):
    hi, lo = halves(x)
    return jnp.concatenate([hi, lo, hi], 1)


def ndot(a, b):
    return lax.dot_general(a, b, (((1,), (1,)), ((), ())), preferred_element_type=F32)


def solve_rows(x, l0, l1):
    return jnp.concatenate([ndot(left3(x[:, :256]), l0), ndot(left3(x), l1)], 1)


def update_kernel(inv, lblk, xcol, xrow, c, fdiag, fpan, out, l0, l1, cols, fs):
    step = pl.program_id(0)
    p, q = lax.axis_index("prow"), lax.axis_index("pcol")
    u, h = step // 2, step % 2

    @pl.when(step == 0)
    def _():
        pair = lblk[pl.ds(pl.multiple_of((p % 2) * 64 + (q // 2) * 8, 8), 8), :]
        fdiag[...] = jnp.where(q % 2 == 0, pair[:4], pair[4:])
        l0[...] = right3(inv[:256, :256])
        l1[...] = right3(inv[256:, :])
        for k in range(4):
            cols[256 * k:256 * (k + 1), :] = right3(solve_rows(xcol[256 * k:256 * (k + 1), :], l0[...], l1[...]))

    f = solve_rows(xrow[...], l0[...], l1[...])
    fs[...] = f

    @pl.when(q // 8 == h)
    def _():
        fpan[0] = fs[pl.ds(pl.multiple_of((q % 8) * 32, 32), 32), :]

    f3 = left3(f)
    for v in range(2):
        present = v * 16 + q <= u * 8 + p

        @pl.when(present)
        def _():
            prod = ndot(f3, cols[512 * v:512 * (v + 1), :])
            for t in range(4):
                at = pl.ds(2 * t + v, 256, stride=8)
                out[at, :] = c[at, :] - prod[:, 128 * t:128 * (t + 1)]

        @pl.when(jnp.logical_not(present))
        def _():
            for t in range(4):
                at = pl.ds(2 * t + v, 256, stride=8)
                out[at, :] = c[at, :]


def update(inv, lblk, xcol, xrow, c):
    whole = lambda s: (0, 0)
    return pl.pallas_call(
        update_kernel,
        grid=(8,),
        in_specs=[
            pl.BlockSpec((512, 512), whole),
            pl.BlockSpec((128, 512), whole),
            pl.BlockSpec((1024, 512), whole),
            pl.BlockSpec((256, 512), lambda s: (s, 0)),
            pl.BlockSpec((2048, 128), lambda s: (s, 0)),
        ],
        out_specs=[
            pl.BlockSpec((4, 512), whole),
            pl.BlockSpec((1, 32, 512), lambda s: (s // 2, 0, 0)),
            pl.BlockSpec((2048, 128), lambda s: (s, 0)),
        ],
        out_shape=[jax.ShapeDtypeStruct((4, 512), F32), jax.ShapeDtypeStruct((4, 32, 512), F32),
                   jax.ShapeDtypeStruct((16384, 128), F32)],
        scratch_shapes=[pltpu.VMEM((256, 768), BF16), pltpu.VMEM((256, 1536), BF16),
                        pltpu.VMEM((1024, 1536), BF16), pltpu.VMEM((256, 512), F32)],
        compiler_params=pltpu.CompilerParams(vmem_limit_bytes=50 << 20),
        name="panel_update",
    )(inv, lblk, xcol, xrow, c)


def gather_factor_kernel(hooks, d, panel, inv, lblk, xrow, xcol, D, M, T, U, s1s, s1r, s2s, s2r, s3s, s3r, rs, rr, cs, cr, loc):
    p, q = lax.axis_index("prow"), lax.axis_index("pcol")
    y, c, x, z = p // 2, p % 2, q // 4, q % 4

    def at(dx, dy, dz, dc=0):
        return (lax.rem(y + dy, 4) * 2 + lax.rem(c + dc, 2), lax.rem(x + dx, 4) * 4 + lax.rem(z + dz, 4))

    def send(src, dst, ssem, rsem, dev):
        return pltpu.make_async_remote_copy(src_ref=src, dst_ref=dst, send_sem=ssem, recv_sem=rsem, device_id=dev, device_id_type=MESH)

    plane = [(dx, dz) for dx in range(4) for dz in range(4) if dx or dz]
    barrier = pltpu.get_barrier_semaphore()
    for dev in [at(dx, 0, dz) for dx, dz in plane] + [at(0, dy, 0) for dy in (1, 2, 3)] + [at(0, 0, 0, 1)]:
        pl.semaphore_signal(barrier, inc=1, device_id=dev, device_id_type=MESH)
    pl.semaphore_wait(barrier, 19)

    a0 = [send(d.at[0], D.at[y, c, q, 0], s1s.at[k], s1r.at[k], at(dx, 0, dz)) for k, (dx, dz) in enumerate(plane)]
    a1 = [send(d.at[1], D.at[y, c, q, 1], s1s.at[14 + dy], s1r.at[14 + dy], at(0, dy, 0)) for dy in (1, 2, 3)]
    for cp in a1 + a0:
        cp.start()
    D[y, c, q] = d[...]
    own = pltpu.make_async_copy(panel, xrow.at[:, x, z], loc.at[0])
    own.start()
    for cp in a1:
        cp.wait_recv()
    b1 = [send(D.at[:, c, q, 1], D.at[:, c, q, 1], s2s.at[k], s2r.at[k], at(dx, 0, dz)) for k, (dx, dz) in enumerate(plane)]
    for cp in b1:
        cp.start()
    for cp in a0:
        cp.wait_recv()
    b0 = [send(D.at[y, c, :, 0], D.at[y, c, :, 0], s2s.at[14 + dy], s2r.at[14 + dy], at(0, dy, 0)) for dy in (1, 2, 3)]
    for cp in b0:
        cp.start()
    for cp in b1:
        cp.wait_recv()
    c1 = send(D.at[:, c, :, 1], D.at[:, c, :, 1], s3s.at[1], s3r.at[1], at(0, 0, 0, 1))
    c1.start()
    for cp in b0:
        cp.wait_recv()
    c0 = send(D.at[:, c, :, 0], D.at[:, c, :, 0], s3s.at[0], s3r.at[0], at(0, 0, 0, 1))
    c0.start()

    def line(ref, u, first_z, off):
        if first_z:
            return ref.at[u, lax.rem(x + off, 4)]
        return ref.at[u, :, lax.rem(z + off, 4)]

    def shard(u, off):
        if u < 2:
            return xrow.at[u, x, lax.rem(z + off, 4)]
        return xrow.at[u, lax.rem(x + off, 4), z]

    def near(u, n):
        return at(0, 0, n) if u < 2 else at(n, 0, 0)

    def far(u, n):
        return at(n, 0, 0) if u < 2 else at(0, 0, n)

    row = {}
    for u in range(4):
        fwd, back = (1, 3) if u % 2 == 0 else (3, 1)
        mine = panel.at[u]
        spot = xrow.at[u, x, z]
        row[u] = [
            [send(mine, spot, rs.at[u, 0], rr.at[u, 0], near(u, 1)), send(mine, spot, rs.at[u, 1], rr.at[u, 1], near(u, 3))],
            [send(shard(u, back), shard(u, back), rs.at[u, 2], rr.at[u, 2], near(u, fwd))],
            [send(line(xrow, u, u < 2, 0), line(xrow, u, u < 2, 0), rs.at[u, 3], rr.at[u, 3], far(u, 1)),
             send(line(xrow, u, u < 2, 0), line(xrow, u, u < 2, 0), rs.at[u, 4], rr.at[u, 4], far(u, 3))],
            [send(line(xrow, u, u < 2, back), line(xrow, u, u < 2, back), rs.at[u, 5], rr.at[u, 5], far(u, fwd))],
        ]

    def row_start(u, s):
        for cp in row[u][s]:
            cp.start()

    def row_wait(u, s):
        for cp in row[u][s]:
            cp.wait_recv()

    root_p = lax.rem(q, 8)
    same = c == root_p % 2
    lag = lax.rem(y - root_p // 2 + 4, 4)

    def col_line(v, i):
        return line(xcol, v, v == 0, (0, 1, 3, 2)[i])

    def col_copies(v, i, src):
        step = 1 if v == 0 else 3
        return (send(src, col_line(v, i), cs.at[v, i, 0], cr.at[v, i], at(0, step, 0)),
                send(src, col_line(v, i), cs.at[v, i, 1], cr.at[v, i], at(0, 0, 0, 1)))

    def hop_of(v):
        return lag if v == 0 else lax.rem(4 - lag, 4)

    def col_root(v, i):
        @pl.when(jnp.logical_and(same, lag == 0))
        def _():
            src = line(xrow, q // 8 + 2 * v, v == 0, (0, 1, 3, 2)[i])
            for cp in col_copies(v, i, src):
                cp.start()
            pltpu.make_async_copy(src, col_line(v, i), loc.at[1 + 4 * v + i]).start()

    def col_relay(v, i, hop):
        @pl.when(jnp.logical_and(same, hop_of(v) == hop))
        def _():
            nxt, other = col_copies(v, i, col_line(v, i))
            other.wait_recv()
            if hop < 3:
                nxt.start()
            other.start()

    def col_end(v, i):
        nxt, other = col_copies(v, i, col_line(v, i))

        @pl.when(jnp.logical_not(same))
        def _():
            other.wait_recv()

        @pl.when(same)
        def _():
            other.wait_send()

        @pl.when(jnp.logical_and(same, hop_of(v) < 3))
        def _():
            nxt.wait_send()

        @pl.when(jnp.logical_and(same, lag == 0))
        def _():
            pltpu.make_async_copy(col_line(v, i), col_line(v, i), loc.at[1 + 4 * v + i]).wait()

    own.wait()
    c1.wait_recv()
    c0.wait_recv()
    acts = {"rs": row_start, "rw": row_wait, "cr": col_root, "cf": col_relay}

    def run(at_hook):
        for act in hooks.get(at_hook, ()):
            acts[act[0]](*act[1:])

    run("start")
    sub = lax.broadcasted_iota(jnp.int32, (8, 128), 0)
    for g in range(64):
        yy, cc, qq = g // 16, (g // 8) % 2, (2 * g) % 16
        for h in range(2):
            e, o = D[yy, cc, qq, h], D[yy, cc, qq + 1, h]
            M[8 * g:8 * g + 8, 256 * h:256 * h + 128] = jnp.where(sub < 4, e, pltpu.roll(o, 4, 0))
            M[8 * g:8 * g + 8, 256 * h + 128:256 * h + 256] = jnp.where(sub < 4, pltpu.roll(e, 4, 0), o)
    chol_body(M, T, U, run)
    inv[...] = M[...]
    lblk[...] = U[:, pl.ds(pl.multiple_of((p // 2) * 128, 128), 128)].T
    run("end")
    for v in range(2):
        for i in range(4):
            col_end(v, i)
    for cp in a0 + a1 + b0 + b1 + [c0, c1]:
        cp.wait_send()
    for u in range(4):
        for s in range(4):
            for cp in row[u][s]:
                cp.wait_send()


def default_hooks():
    h = {k: [] for k in ["start", "end"] + list(range(16))}
    U4 = range(4)
    h["start"] += [("rs", u, 0) for u in U4]
    h[2] += [a for u in U4 for a in (("rw", u, 0), ("rs", u, 1))]
    h[4] += [a for u in U4 for a in (("rw", u, 1), ("rs", u, 2))]
    h[4] += [("cr", v, 0) for v in range(2)]
    h[7] += [("cf", v, 0, 1) for v in range(2)]
    h[9] += [("cf", v, 0, 2) for v in range(2)]
    h[10] += [a for u in (0, 2) for a in (("rw", u, 2), ("rs", u, 3))]
    h[11] += [("cf", v, 0, 3) for v in range(2)]
    h[13] += [a for u in (1, 3) for a in (("rw", u, 2), ("rs", u, 3))]
    h[13] += [("cr", v, i) for i in (1, 2) for v in range(2)]
    h["end"] += [("cf", v, i, 1) for i in (1, 2) for v in range(2)]
    h["end"] += [("rw", u, 3) for u in U4]
    h["end"] += [("cr", v, 3) for v in range(2)]
    h["end"] += [("cf", v, i, 2) for i in (1, 2) for v in range(2)]
    h["end"] += [("cf", v, 3, 1) for v in range(2)]
    h["end"] += [("cf", v, i, 3) for i in (1, 2) for v in range(2)]
    h["end"] += [("cf", v, 3, 2) for v in range(2)]
    h["end"] += [("cf", v, 3, 3) for v in range(2)]
    return h


def gather_factor(d, panel):
    dma = pltpu.SemaphoreType.DMA
    anywhere = pl.BlockSpec(memory_space=pl.ANY)
    vmem = pl.BlockSpec(memory_space=pltpu.VMEM)
    return pl.pallas_call(
        functools.partial(gather_factor_kernel, default_hooks()),
        out_shape=[jax.ShapeDtypeStruct((512, 512), F32), jax.ShapeDtypeStruct((128, 512), F32),
                   jax.ShapeDtypeStruct((4, 4, 4, 32, 512), F32), jax.ShapeDtypeStruct((2, 4, 4, 32, 512), F32)],
        in_specs=[vmem, anywhere],
        out_specs=[vmem, vmem, anywhere, anywhere],
        scratch_shapes=[pltpu.VMEM((4, 2, 16, 2, 8, 128), F32), pltpu.VMEM((512, 512), F32), pltpu.VMEM((128, 256), F32),
                        pltpu.VMEM((512, 512), F32), dma((18,)), dma((18,)), dma((18,)), dma((18,)), dma((2,)), dma((2,)),
                        dma((4, 6)), dma((4, 6)), dma((2, 4, 2)), dma((2, 4)), dma((9,))],
        compiler_params=pltpu.CompilerParams(collective_id=0, has_side_effects=True, vmem_limit_bytes=40 << 20),
        name="gather_factor",
    )(d, panel)


def per_device(diag_block, panel, trailing):
    d = diag_block.reshape(4, 4, 128).transpose(1, 0, 2).reshape(2, 8, 128)
    inv, lblk, xrow, xcol = gather_factor(d, panel)
    c = trailing.reshape(4, 512, 2, 4, 128).transpose(0, 1, 3, 2, 4).reshape(16384, 128)
    factor_diag, factor_panel, out = update(inv, lblk, xcol.reshape(1024, 512), xrow.reshape(2048, 512), c)
    updated = out.reshape(4, 512, 4, 2, 128).transpose(0, 1, 3, 2, 4).reshape(4, 512, 2, 512)
    return factor_diag, factor_panel, updated


def solution(mesh):
    specs = (P(("prow", "pcol"), None), P(None, ("prow", "pcol"), None), P(None, "prow", None, "pcol"))
    return jax.shard_map(per_device, mesh=mesh, in_specs=specs, out_specs=specs, check_vma=False)
```

```python
import functools

import jax
import jax.numpy as jnp
from jax import lax
from jax.experimental import pallas as pl
from jax.experimental.pallas import tpu as pltpu
from jax.sharding import PartitionSpec as P

F32 = jnp.float32
BF16 = jnp.bfloat16
HI = lax.Precision.HIGHEST
MESH = pl.DeviceIdType.MESH


def tdot(a, b, prec=HI):
    return lax.dot_general(a, b, (((0,), (0,)), ((), ())), precision=prec, preferred_element_type=F32)

def bc(col, n=128):
    return jnp.broadcast_to(col, (col.shape[0], n))

def elim8(G, c0, sub):
    n = len(G)
    C = [[bc(G[g][:, c0 + j:c0 + j + 1]) for j in range(8)] for g in range(n)]
    L = [G[g][:, :128] for g in range(n)]
    V = [G[g][:, 128:] for g in range(n)]
    dv = None
    for j in range(8):
        piv = [jnp.broadcast_to(C[0][l][j:j + 1, :], (8, 128)) for l in range(j, 8)]
        rinv = 1.0 / piv[0]
        rowL = jnp.broadcast_to(L[0][j:j + 1, :], (8, 128))
        rowV = jnp.broadcast_to(V[0][j:j + 1, :], (8, 128))
        dv = piv[0] if j == 0 else jnp.where(sub == j, piv[0], dv)
        for g in range(n):
            m = C[g][j] * rinv
            if g == 0:
                m = jnp.where(sub > j, m, 0.0)
            for l in range(j + 1, 8):
                C[g][l] = C[g][l] - m * piv[l - j]
            L[g] = L[g] - m * rowL
            V[g] = V[g] - m * rowV
    sc = lax.rsqrt(dv)
    L[0] = L[0] * sc
    V[0] = V[0] * sc
    return [jnp.concatenate([L[g], V[g]], 1) for g in range(n)]

def leaf(T, hook, k):
    sub = lax.broadcasted_iota(jnp.int32, (8, 128), 0)
    for sb in range(4):
        r0 = 32 * sb
        G = [T[r0 + 8 * g:r0 + 8 * g + 8, :] for g in range(4)]
        done = []
        for g in range(4):
            G = elim8(G, r0 + 8 * g, sub)
            done.append(G[0])
            T[r0 + 8 * g:r0 + 8 * g + 8, :] = G[0]
            G = G[1:]
        hook(4 * k + sb)
        if sb < 3:
            W = jnp.concatenate(done, 0)
            Pm = tdot(W[:, :128], W)
            T[r0 + 32:128, :] = T[r0 + 32:128, :] - Pm[r0 + 32:128, :]

def chol_body(M, T, U, hook, nb=4):
    row = lax.broadcasted_iota(jnp.int32, (128, 128), 0)
    col = lax.broadcasted_iota(jnp.int32, (128, 128), 1)
    eye = jnp.where(row == col, 1.0, 0.0).astype(F32)
    n = nb * 128
    for k in range(nb):
        a, b = k * 128, (k + 1) * 128
        T[:, :128] = M[a:b, a:b]
        T[:, 128:] = eye
        leaf(T, hook, k)
        Ukk = jnp.where(col >= row, T[:, :128], 0.0)
        Vkk = jnp.where(col <= row, T[:, 128:], 0.0)
        U[a:b, a:b] = Ukk
        if k > 0:
            U[a:b, :a] = jnp.zeros((128, a), F32)
            M[a:b, :a] = jnp.dot(Vkk, M[a:b, :a], precision=HI, preferred_element_type=F32)
        M[a:b, a:b] = Vkk
        if k < nb - 1:
            Ur = jnp.dot(Vkk, M[a:b, b:], precision=HI, preferred_element_type=F32)
            U[a:b, b:] = Ur
            M[a:b, b:] = jnp.zeros((128, n - b), F32)
            if k > 0:
                M[b:, :a] = M[b:, :a] - tdot(Ur, M[a:b, :a])
            M[b:, a:b] = -tdot(Ur, Vkk)
            M[b:, b:] = M[b:, b:] - tdot(Ur, Ur)


def halves(x):
    hi = x.astype(BF16)
    return hi, (x - hi.astype(F32)).astype(BF16)


def left3(x):
    hi, lo = halves(x)
    return jnp.concatenate([hi, hi, lo], 1)


def right3(x):
    hi, lo = halves(x)
    return jnp.concatenate([hi, lo, hi], 0)


def bdot(a, b):
    return jnp.dot(a, b, preferred_element_type=F32)


def solve_rows(x, l0, l1):
    return jnp.concatenate([bdot(left3(x[:, :256]), l0), bdot(left3(x), l1)], 1)


ROWS = 256


def update_kernel(inv, lblk, xcol, xrow, c, fdiag, fpan, out, l0, l1, cols, fs, made, sems):
    p, q = lax.axis_index("prow"), lax.axis_index("pcol")
    pair = lblk[pl.ds(pl.multiple_of((p % 2) * 64 + (q // 2) * 8, 8), 8), :]
    fdiag[...] = jnp.where(q % 2 == 0, pair[:4], pair[4:])
    l0[...] = right3(inv[:256, :256].T)
    l1[...] = right3(inv[256:, :].T)
    for k in range(4):
        f = solve_rows(xcol[256 * k:256 * (k + 1), :], l0[...], l1[...])
        cols[:, 256 * k:256 * (k + 1)] = right3(f.T)

    copies = []
    for u in range(4):
        f = solve_rows(xrow[512 * u:512 * (u + 1), :], l0[...], l1[...])
        fs[...] = f
        fpan[u] = fs[pl.ds(pl.multiple_of(q * 32, 32), 32), :]
        f3 = left3(f)

        def product(v, r):
            prod = bdot(f3[r:r + ROWS], cols[:, 512 * v:512 * (v + 1)])
            for t in range(4):
                at = pl.ds(8 * (512 * u + r) + 2 * t + v, ROWS, stride=8)
                made[at, :] = c[at, :] - prod[:, 128 * t:128 * (t + 1)]

        def keep(v, r):
            for t in range(4):
                at = pl.ds(8 * (512 * u + r) + 2 * t + v, ROWS, stride=8)
                made[at, :] = c[at, :]

        def both(v, r):
            present = v * 16 + q <= u * 8 + p
            pl.when(present)(functools.partial(product, v, r))
            pl.when(jnp.logical_not(present))(functools.partial(keep, v, r))

        for r in range(0, 512, ROWS):
            for v in range(2):
                if v == u // 2:
                    both(v, r)
                elif v < u // 2:
                    product(v, r)
                else:
                    keep(v, r)
            at = pl.ds(8 * (512 * u + r), 8 * ROWS)
            cp = pltpu.make_async_copy(made.at[at], out.at[at], sems.at[len(copies)])
            cp.start()
            copies.append(cp)
    for cp in copies:
        cp.wait()


def update(inv, lblk, xcol, xrow, c):
    vmem = pl.BlockSpec(memory_space=pltpu.VMEM)
    return pl.pallas_call(
        update_kernel,
        in_specs=[vmem] * 5,
        out_specs=[vmem, vmem, pl.BlockSpec(memory_space=pltpu.HBM)],
        out_shape=[jax.ShapeDtypeStruct((4, 512), F32), jax.ShapeDtypeStruct((4, 32, 512), F32),
                   jax.ShapeDtypeStruct((16384, 128), F32)],
        scratch_shapes=[pltpu.VMEM((768, 256), BF16), pltpu.VMEM((1536, 256), BF16), pltpu.VMEM((1536, 1024), BF16),
                        pltpu.VMEM((512, 512), F32), pltpu.VMEM((16384, 128), F32), pltpu.SemaphoreType.DMA((2048 // ROWS,))],
        compiler_params=pltpu.CompilerParams(vmem_limit_bytes=26 << 20),
        name="panel_update",
    )(inv, lblk, xcol, xrow, c)


def gather_factor_kernel(hooks, d, panel, inv, lblk, xrow, xcol, D, M, T, U, s1s, s1r, s2s, s2r, s3s, s3r, rs, rr, cs, cr, loc):
    p, q = lax.axis_index("prow"), lax.axis_index("pcol")
    y, c, x, z = p // 2, p % 2, q // 4, q % 4

    def at(dx, dy, dz, dc=0):
        return (lax.rem(y + dy, 4) * 2 + lax.rem(c + dc, 2), lax.rem(x + dx, 4) * 4 + lax.rem(z + dz, 4))

    def send(src, dst, ssem, rsem, dev):
        return pltpu.make_async_remote_copy(src_ref=src, dst_ref=dst, send_sem=ssem, recv_sem=rsem, device_id=dev, device_id_type=MESH)

    plane = [(dx, dz) for dx in range(4) for dz in range(4) if dx or dz]
    barrier = pltpu.get_barrier_semaphore()
    for dev in [at(dx, 0, dz) for dx, dz in plane] + [at(0, dy, 0) for dy in (1, 2, 3)] + [at(0, 0, 0, 1)]:
        pl.semaphore_signal(barrier, inc=1, device_id=dev, device_id_type=MESH)
    pl.semaphore_wait(barrier, 19)

    a0 = [send(d.at[0], D.at[0, y, c, q], s1s.at[k], s1r.at[k], at(dx, 0, dz)) for k, (dx, dz) in enumerate(plane)]
    a1 = [send(d.at[1], D.at[1, y, c, q], s1s.at[14 + dy], s1r.at[14 + dy], at(0, dy, 0)) for dy in (1, 2, 3)]
    for cp in a1 + a0:
        cp.start()
    dloc = pltpu.make_async_copy(d, D.at[:, y, c, q], loc.at[3])
    dloc.start()
    own = pltpu.make_async_copy(panel, xrow.at[:, :, x, z], loc.at[0])
    own.start()
    for cp in a1:
        cp.wait_recv()
    dloc.wait()
    b1 = [send(D.at[1, :, c, q], D.at[1, :, c, q], s2s.at[k], s2r.at[k], at(dx, 0, dz)) for k, (dx, dz) in enumerate(plane)]
    for cp in b1:
        cp.start()
    for cp in a0:
        cp.wait_recv()
    b0 = [send(D.at[0, y, c], D.at[0, y, c], s2s.at[14 + dy], s2r.at[14 + dy], at(0, dy, 0)) for dy in (1, 2, 3)]
    for cp in b0:
        cp.start()

    mate, away = 1 + 2 * lax.rem(x, 2), 3 - 2 * lax.rem(x, 2)
    first = x // 2

    def near(w, n):
        return at(0, 0, n) if w == 0 else at(n, 0, 0)

    def line(ref, w, off):
        if w == 0:
            return ref.at[lax.rem(x + off, 4)]
        return ref.at[:, lax.rem(z + off, 4)]

    ra = [send(panel.at[w], xrow.at[w, :, x, z], rs.at[3 * w + n - 1], rr.at[3 * w + n - 1], near(w, n)) for n in (1, 3, 2) for w in (0, 1)]

    def pick(w, n, k):
        u = lax.rem(x + n, 4) // 2 if w == 0 else first
        return xrow.at[w, u if k == 0 else 1 - u]

    rb, rc = {}, {}
    for w in (0, 1):
        for k in (0, 1):
            j = 6 + 3 * (2 * w + k)
            rb[w, k] = []
            for s, n in enumerate((1, 3)):
                ref = line(pick(w, n, k), w, 0)
                rb[w, k].append(send(ref, ref, rs.at[j + s], rr.at[j + s], at(n, 0, 0) if w == 0 else at(0, 0, n)))
            if w == 0:
                ref = line(xrow.at[0, first], 0, away if k == 0 else mate)
                rc[w, k] = send(ref, ref, rs.at[j + 2], rr.at[j + 2], at(mate if k == 0 else away, 0, 0))
            else:
                ref = line(xrow.at[1, first if k == 0 else 1 - first], 1, 3 if k == 0 else 1)
                rc[w, k] = send(ref, ref, rs.at[j + 2], rr.at[j + 2], at(0, 0, 1 if k == 0 else 3))

    lag = lax.rem(y - lax.rem(q, 8) // 2 + 4, 4)
    same = c == lax.rem(q, 2)
    is_root = p == lax.rem(q, 8)

    def chunk(ref, v, i):
        off, part = CHUNKS[i]
        ref = line(ref, v, off)
        return ref if part is None else ref.at[pl.ds(2 * part, 2)]

    def chain(src, v, i):
        part, spot = chunk(src, v, i), chunk(xcol.at[v], v, i)
        return (send(part, spot, cs.at[v, i, 0], cr.at[v, i], at(0, 1 if v == 0 else 3, 0)),
                send(part, spot, cs.at[v, i, 1], cr.at[v, i], at(0, 0, 0, 1)))

    def hop_of(v):
        return lag if v == 0 else lax.rem(4 - lag, 4)

    def col_root(*chunks):
        @pl.when(is_root)
        def _():
            both = [chain(xrow.at[v, first], v, i) for i in chunks for v in range(2)]
            for nxt, other in both:
                nxt.start()
            for nxt, other in both:
                other.start()

    def col_local():
        @pl.when(is_root)
        def _():
            for v in range(2):
                pltpu.make_async_copy(xrow.at[v, first], xcol.at[v], loc.at[1 + v]).start()

    def col_hop(i, hop):
        for v in range(2):
            @pl.when(jnp.logical_and(same, hop_of(v) == hop))
            def _():
                nxt, other = chain(xcol.at[v], v, i)
                other.wait_recv()
                if hop < 3:
                    nxt.start()
                other.start()

    def col_end():
        for v in range(2):
            for i in range(len(CHUNKS)):
                nxt, other = chain(xcol.at[v], v, i)
                pl.when(jnp.logical_not(same))(other.wait_recv)
                pl.when(same)(other.wait_send)
                pl.when(jnp.logical_and(same, hop_of(v) < 3))(nxt.wait_send)

            @pl.when(is_root)
            def _():
                pltpu.make_async_copy(xrow.at[v, first], xcol.at[v], loc.at[1 + v]).wait()

    def row_a_start():
        for cp in ra:
            cp.start()

    def row_a():
        for cp in ra:
            cp.wait_recv()
        for w in (0, 1):
            for cp in rb[w, 0]:
                cp.start()

    def row_b0():
        for w in (0, 1):
            for cp in rb[w, 0]:
                cp.wait_recv()
            rc[w, 0].start()
        rc[0, 1].start()
        for w in (0, 1):
            for cp in rb[w, 1]:
                cp.start()

    def row_c0():
        for w in (0, 1):
            rc[w, 0].wait_recv()

    def row_b1():
        for cp in rb[1, 1]:
            cp.wait_recv()
        rc[1, 1].start()

    def row_c1():
        for cp in rb[0, 1] + [rc[0, 1], rc[1, 1]]:
            cp.wait_recv()

    acts = {"as": row_a_start, "a": row_a, "b0": row_b0, "c0": row_c0, "b1": row_b1, "c1": row_c1,
            "root": col_root, "local": col_local, "hop": col_hop}

    def run(where):
        for act in hooks.get(where, ()):
            acts[act[0]](*act[1:])

    run("first")
    for cp in b1:
        cp.wait_recv()
    c1 = send(D.at[1, :, c], D.at[1, :, c], s3s.at[1], s3r.at[1], at(0, 0, 0, 1))
    c1.start()
    for cp in b0:
        cp.wait_recv()
    c0 = send(D.at[0, :, c], D.at[0, :, c], s3s.at[0], s3r.at[0], at(0, 0, 0, 1))
    c0.start()
    own.wait()
    run("second")
    c1.wait_recv()
    c0.wait_recv()
    run("start")
    sub = lax.broadcasted_iota(jnp.int32, (8, 128), 0)
    for g in range(64):
        yy, cc, qq = g // 16, (g // 8) % 2, (2 * g) % 16
        for h in range(2):
            e, o = D[h, yy, cc, qq], D[h, yy, cc, qq + 1]
            M[8 * g:8 * g + 8, 256 * h:256 * h + 128] = jnp.where(sub < 4, e, pltpu.roll(o, 4, 0))
            M[8 * g:8 * g + 8, 256 * h + 128:256 * h + 256] = jnp.where(sub < 4, pltpu.roll(e, 4, 0), o)
    chol_body(M, T, U, run)
    inv[...] = M[...]
    lblk[...] = U[:, pl.ds(pl.multiple_of((p // 2) * 128, 128), 128)].T
    run("end")
    col_end()
    for cp in a0 + a1 + b0 + b1 + [c0, c1] + ra + [cp for k in rb for cp in rb[k]] + list(rc.values()):
        cp.wait_send()


CHUNKS = ((0, None), (1, None), (3, None), (2, 0), (2, 1))


def default_hooks():
    return {
        "first": [("as",)],
        "second": [("a",), ("root", 0)],
        "start": [("hop", 0, 1)],
        0: [("b0",), ("root", 1, 2)],
        2: [("hop", 0, 2)],
        4: [("hop", 1, 1)],
        6: [("c0",), ("root", 3, 4), ("local",), ("hop", 2, 1), ("hop", 0, 3)],
        7: [("hop", 1, 2), ("b1",)],
        8: [("hop", 3, 1)],
        9: [("hop", 4, 1), ("hop", 2, 2)],
        11: [("hop", 3, 2), ("hop", 1, 3)],
        12: [("hop", 4, 2)],
        13: [("hop", 2, 3)],
        14: [("hop", 3, 3)],
        "end": [("hop", 4, 3), ("c1",)],
    }


def gather_factor(d, panel):
    dma = pltpu.SemaphoreType.DMA
    vmem = pl.BlockSpec(memory_space=pltpu.VMEM)
    return pl.pallas_call(
        functools.partial(gather_factor_kernel, default_hooks()),
        out_shape=[jax.ShapeDtypeStruct((512, 512), F32), jax.ShapeDtypeStruct((128, 512), F32),
                   jax.ShapeDtypeStruct((2, 2, 4, 4, 32, 512), F32), jax.ShapeDtypeStruct((2, 4, 4, 32, 512), F32)],
        in_specs=[pl.BlockSpec(memory_space=pl.ANY)] * 2,
        out_specs=[vmem] * 4,
        scratch_shapes=[pltpu.VMEM((2, 4, 2, 16, 8, 128), F32), pltpu.VMEM((512, 512), F32), pltpu.VMEM((128, 256), F32),
                        pltpu.VMEM((512, 512), F32), dma((18,)), dma((18,)), dma((18,)), dma((18,)), dma((2,)), dma((2,)),
                        dma((18,)), dma((18,)), dma((2, 5, 2)), dma((2, 5)), dma((4,))],
        compiler_params=pltpu.CompilerParams(collective_id=0, has_side_effects=True, vmem_limit_bytes=24 << 20),
        cost_estimate=pl.CostEstimate(flops=4 * 10**10, bytes_accessed=80 << 20, transcendentals=0),
        name="gather_factor",
    )(d, panel)


def per_device(diag_block, panel, trailing):
    d = diag_block.reshape(4, 4, 128).transpose(1, 0, 2).reshape(2, 8, 128)
    inv, lblk, xrow, xcol = gather_factor(d, panel.reshape(2, 2, 32, 512))
    c = trailing.reshape(4, 512, 2, 4, 128).transpose(0, 1, 3, 2, 4).reshape(16384, 128)
    factor_diag, factor_panel, out = update(inv, lblk, xcol.reshape(1024, 512), xrow.reshape(2048, 512), c)
    updated = out.reshape(4, 512, 4, 2, 128).transpose(0, 1, 3, 2, 4).reshape(4, 512, 2, 512)
    return factor_diag, factor_panel, updated


def solution(mesh):
    specs = (P(("prow", "pcol"), None), P(None, ("prow", "pcol"), None), P(None, "prow", None, "pcol"))
    return jax.shard_map(per_device, mesh=mesh, in_specs=specs, out_specs=specs, check_vma=False)
```

```python
import functools

import jax
import jax.numpy as jnp
from jax import lax
from jax.experimental import pallas as pl
from jax.experimental.pallas import tpu as pltpu
from jax.sharding import PartitionSpec as P

F32 = jnp.float32
BF16 = jnp.bfloat16
HI = lax.Precision.HIGHEST
MESH = pl.DeviceIdType.MESH


def tdot(a, b, prec=HI):
    return lax.dot_general(a, b, (((0,), (0,)), ((), ())), precision=prec, preferred_element_type=F32)

def bc(col, n=128):
    return jnp.broadcast_to(col, (col.shape[0], n))

def elim8(G, c0, sub):
    n = len(G)
    C = [[bc(G[g][:, c0 + j:c0 + j + 1]) for j in range(8)] for g in range(n)]
    L = [G[g][:, :128] for g in range(n)]
    V = [G[g][:, 128:] for g in range(n)]
    dv = None
    for j in range(8):
        piv = [jnp.broadcast_to(C[0][l][j:j + 1, :], (8, 128)) for l in range(j, 8)]
        rinv = 1.0 / piv[0]
        rowL = jnp.broadcast_to(L[0][j:j + 1, :], (8, 128))
        rowV = jnp.broadcast_to(V[0][j:j + 1, :], (8, 128))
        dv = piv[0] if j == 0 else jnp.where(sub == j, piv[0], dv)
        for g in range(n):
            m = C[g][j] * rinv
            if g == 0:
                m = jnp.where(sub > j, m, 0.0)
            for l in range(j + 1, 8):
                C[g][l] = C[g][l] - m * piv[l - j]
            L[g] = L[g] - m * rowL
            V[g] = V[g] - m * rowV
    sc = lax.rsqrt(dv)
    L[0] = L[0] * sc
    V[0] = V[0] * sc
    return [jnp.concatenate([L[g], V[g]], 1) for g in range(n)]

def leaf(T, hook, k):
    sub = lax.broadcasted_iota(jnp.int32, (8, 128), 0)
    for sb in range(4):
        r0 = 32 * sb
        G = [T[r0 + 8 * g:r0 + 8 * g + 8, :] for g in range(4)]
        done = []
        for g in range(4):
            G = elim8(G, r0 + 8 * g, sub)
            done.append(G[0])
            T[r0 + 8 * g:r0 + 8 * g + 8, :] = G[0]
            G = G[1:]
        hook(4 * k + sb)
        if sb < 3:
            W = jnp.concatenate(done, 0)
            Pm = tdot(W[:, :128], W)
            T[r0 + 32:128, :] = T[r0 + 32:128, :] - Pm[r0 + 32:128, :]

def chol_body(M, T, U, hook, nb=4):
    row = lax.broadcasted_iota(jnp.int32, (128, 128), 0)
    col = lax.broadcasted_iota(jnp.int32, (128, 128), 1)
    eye = jnp.where(row == col, 1.0, 0.0).astype(F32)
    n = nb * 128
    for k in range(nb):
        a, b = k * 128, (k + 1) * 128
        T[:, :128] = M[a:b, a:b]
        T[:, 128:] = eye
        leaf(T, hook, k)
        Ukk = jnp.where(col >= row, T[:, :128], 0.0)
        Vkk = jnp.where(col <= row, T[:, 128:], 0.0)
        U[a:b, a:b] = Ukk
        if k > 0:
            U[a:b, :a] = jnp.zeros((128, a), F32)
            M[a:b, :a] = jnp.dot(Vkk, M[a:b, :a], precision=HI, preferred_element_type=F32)
        M[a:b, a:b] = Vkk
        if k < nb - 1:
            Ur = jnp.dot(Vkk, M[a:b, b:], precision=HI, preferred_element_type=F32)
            U[a:b, b:] = Ur
            M[a:b, b:] = jnp.zeros((128, n - b), F32)
            if k > 0:
                M[b:, :a] = M[b:, :a] - tdot(Ur, M[a:b, :a])
            M[b:, a:b] = -tdot(Ur, Vkk)
            M[b:, b:] = M[b:, b:] - tdot(Ur, Ur)


def halves(x):
    hi = x.astype(BF16)
    return hi, (x - hi.astype(F32)).astype(BF16)


def left3(x):
    hi, lo = halves(x)
    return jnp.concatenate([hi, hi, lo], 1)


def right3(x):
    hi, lo = halves(x)
    return jnp.concatenate([hi, lo, hi], 0)


def bdot(a, b):
    return jnp.dot(a, b, preferred_element_type=F32)


def solve_rows(x, l0, l1):
    return jnp.concatenate([bdot(left3(x[:, :256]), l0), bdot(left3(x), l1)], 1)


ROWS = 256


def update_kernel(lblk, l0, l1, fhi, flo, frows, xcol, c, fdiag, fpan, out, cols, made, sems):
    p, q = lax.axis_index("prow"), lax.axis_index("pcol")
    pair = lblk[pl.ds(pl.multiple_of((p % 2) * 64 + (q // 2) * 8, 8), 8), :]
    fdiag[...] = jnp.where(q % 2 == 0, pair[:4], pair[4:])
    fpan[...] = frows[...]
    for k in range(4):
        f = solve_rows(xcol[256 * k:256 * (k + 1), :], l0[...], l1[...])
        cols[:, 256 * k:256 * (k + 1)] = right3(f.T)

    copies = []
    for u in range(4):
        f3 = jnp.concatenate([fhi[u], fhi[u], flo[u]], 1)

        def product(v, r):
            prod = bdot(f3[r:r + ROWS], cols[:, 512 * v:512 * (v + 1)])
            for t in range(4):
                at = pl.ds(8 * (512 * u + r) + 2 * t + v, ROWS, stride=8)
                made[at, :] = c[at, :] - prod[:, 128 * t:128 * (t + 1)]

        def keep(v, r):
            for t in range(4):
                at = pl.ds(8 * (512 * u + r) + 2 * t + v, ROWS, stride=8)
                made[at, :] = c[at, :]

        def both(v, r):
            present = v * 16 + q <= u * 8 + p
            pl.when(present)(functools.partial(product, v, r))
            pl.when(jnp.logical_not(present))(functools.partial(keep, v, r))

        for r in range(0, 512, ROWS):
            for v in range(2):
                if v == u // 2:
                    both(v, r)
                elif v < u // 2:
                    product(v, r)
                else:
                    keep(v, r)
            at = pl.ds(8 * (512 * u + r), 8 * ROWS)
            cp = pltpu.make_async_copy(made.at[at], out.at[at], sems.at[len(copies)])
            cp.start()
            copies.append(cp)
    for cp in copies:
        cp.wait()


def update(lblk, l0, l1, fhi, flo, frows, xcol, c):
    vmem = pl.BlockSpec(memory_space=pltpu.VMEM)
    return pl.pallas_call(
        update_kernel,
        in_specs=[vmem] * 8,
        out_specs=[vmem, vmem, pl.BlockSpec(memory_space=pltpu.HBM)],
        out_shape=[jax.ShapeDtypeStruct((4, 512), F32), jax.ShapeDtypeStruct((4, 32, 512), F32),
                   jax.ShapeDtypeStruct((16384, 128), F32)],
        scratch_shapes=[pltpu.VMEM((1536, 1024), BF16), pltpu.VMEM((16384, 128), F32), pltpu.SemaphoreType.DMA((2048 // ROWS,))],
        compiler_params=pltpu.CompilerParams(vmem_limit_bytes=26 << 20),
        name="panel_update",
    )(lblk, l0, l1, fhi, flo, frows, xcol, c)


def gather_factor_kernel(hooks, d, panel, lblk, l0, l1, fhi, flo, fpan, xcol, xrow, fs, D, M, T, U, s1s, s1r, s2s, s2r, s3s, s3r, rs, rr, cs, cr, loc):
    p, q = lax.axis_index("prow"), lax.axis_index("pcol")
    y, c, x, z = p // 2, p % 2, q // 4, q % 4

    def at(dx, dy, dz, dc=0):
        return (lax.rem(y + dy, 4) * 2 + lax.rem(c + dc, 2), lax.rem(x + dx, 4) * 4 + lax.rem(z + dz, 4))

    def send(src, dst, ssem, rsem, dev):
        return pltpu.make_async_remote_copy(src_ref=src, dst_ref=dst, send_sem=ssem, recv_sem=rsem, device_id=dev, device_id_type=MESH)

    plane = [(dx, dz) for dx in range(4) for dz in range(4) if dx or dz]
    barrier = pltpu.get_barrier_semaphore()
    for dev in [at(dx, 0, dz) for dx, dz in plane] + [at(0, dy, 0) for dy in (1, 2, 3)] + [at(0, 0, 0, 1)]:
        pl.semaphore_signal(barrier, inc=1, device_id=dev, device_id_type=MESH)
    pl.semaphore_wait(barrier, 19)

    a0 = [send(d.at[0], D.at[0, y, c, q], s1s.at[k], s1r.at[k], at(dx, 0, dz)) for k, (dx, dz) in enumerate(plane)]
    a1 = [send(d.at[1], D.at[1, y, c, q], s1s.at[14 + dy], s1r.at[14 + dy], at(0, dy, 0)) for dy in (1, 2, 3)]
    for cp in a1 + a0:
        cp.start()
    dloc = pltpu.make_async_copy(d, D.at[:, y, c, q], loc.at[3])
    dloc.start()
    own = pltpu.make_async_copy(panel, xrow.at[:, :, x, z], loc.at[0])
    own.start()
    for cp in a1:
        cp.wait_recv()
    dloc.wait()
    b1 = [send(D.at[1, :, c, q], D.at[1, :, c, q], s2s.at[k], s2r.at[k], at(dx, 0, dz)) for k, (dx, dz) in enumerate(plane)]
    for cp in b1:
        cp.start()
    for cp in a0:
        cp.wait_recv()
    b0 = [send(D.at[0, y, c], D.at[0, y, c], s2s.at[14 + dy], s2r.at[14 + dy], at(0, dy, 0)) for dy in (1, 2, 3)]
    for cp in b0:
        cp.start()

    first = x // 2

    def place(w):
        return x if w == 0 else z

    def prior(w, n):
        there = lax.rem(place(w) + n, 4) // 2
        return there if w == 0 else lax.rem(first + there + lax.rem(p, 4) // 2, 2)

    def near(w, n):
        return at(0, 0, n) if w == 0 else at(n, 0, 0)

    def line(ref, w, off):
        if w == 0:
            return ref.at[lax.rem(x + off, 4)]
        return ref.at[:, lax.rem(z + off, 4)]

    ra = [send(panel.at[w], xrow.at[w, :, x, z], rs.at[3 * w + n - 1], rr.at[3 * w + n - 1], near(w, n)) for n in (1, 3, 2) for w in (0, 1)]

    def pick(w, n, k):
        u = prior(w, n)
        return xrow.at[w, u if k == 0 else 1 - u]

    def along(w, n):
        return at(n, 0, 0) if w == 0 else at(0, 0, n)

    rb, rc = {}, {}
    for w in (0, 1):
        mate, away = 1 + 2 * lax.rem(place(w), 2), 3 - 2 * lax.rem(place(w), 2)
        for k in (0, 1):
            j = 6 + 3 * (2 * w + k)
            rb[w, k] = []
            for s, n in enumerate((1, 3)):
                ref = line(pick(w, n, k), w, 0)
                rb[w, k].append(send(ref, ref, rs.at[j + s], rr.at[j + s], along(w, n)))
            ref = line(pick(w, 0, 0), w, away if k == 0 else mate)
            rc[w, k] = send(ref, ref, rs.at[j + 2], rr.at[j + 2], along(w, mate if k == 0 else away))

    lag = lax.rem(y - lax.rem(q, 8) // 2 + 4, 4)
    same = c == lax.rem(q, 2)
    is_root = p == lax.rem(q, 8)

    def chunk(ref, v, i):
        off, part = CHUNKS[i]
        ref = line(ref, v, off)
        return ref if part is None else ref.at[pl.ds(2 * part, 2)]

    def chain(src, v, i):
        part, spot = chunk(src, v, i), chunk(xcol.at[v], v, i)
        return (send(part, spot, cs.at[v, i, 0], cr.at[v, i], at(0, 1 if v == 0 else 3, 0)),
                send(part, spot, cs.at[v, i, 1], cr.at[v, i], at(0, 0, 0, 1)))

    def hop_of(v):
        return lag if v == 0 else lax.rem(4 - lag, 4)

    def col_root(*chunks):
        @pl.when(is_root)
        def _():
            both = [chain(xrow.at[v, first], v, i) for i in chunks for v in range(2)]
            for nxt, other in both:
                nxt.start()
            for nxt, other in both:
                other.start()

    def col_local():
        @pl.when(is_root)
        def _():
            for v in range(2):
                pltpu.make_async_copy(xrow.at[v, first], xcol.at[v], loc.at[1 + v]).start()

    def col_hop(i, hop):
        for v in range(2):
            @pl.when(jnp.logical_and(same, hop_of(v) == hop))
            def _():
                nxt, other = chain(xcol.at[v], v, i)
                other.wait_recv()
                if hop < 3:
                    nxt.start()
                other.start()

    def col_end():
        for v in range(2):
            for i in range(len(CHUNKS)):
                nxt, other = chain(xcol.at[v], v, i)
                pl.when(jnp.logical_not(same))(other.wait_recv)
                pl.when(same)(other.wait_send)
                pl.when(jnp.logical_and(same, hop_of(v) < 3))(nxt.wait_send)

            @pl.when(is_root)
            def _():
                pltpu.make_async_copy(xrow.at[v, first], xcol.at[v], loc.at[1 + v]).wait()

    def row_a_start():
        for cp in ra:
            cp.start()

    def row_a():
        for cp in ra:
            cp.wait_recv()
        for w in (0, 1):
            for cp in rb[w, 0]:
                cp.start()

    def row_b0():
        for w in (0, 1):
            for cp in rb[w, 0]:
                cp.wait_recv()
            rc[w, 0].start()

    def row_b1():
        for w in (0, 1):
            rc[w, 1].start()
            for cp in rb[w, 1]:
                cp.start()

    def row_c0():
        for w in (0, 1):
            rc[w, 0].wait_recv()

    def row_c1():
        for w in (0, 1):
            for cp in rb[w, 1] + [rc[w, 1]]:
                cp.wait_recv()

    def solve(w, k):
        u = prior(w, 0) if k == 0 else 1 - prior(w, 0)
        f = solve_rows(xrow[w, u].reshape(512, 512), l0[...], l1[...])
        fs[...] = f
        fpan[2 * w + u] = fs[pl.ds(pl.multiple_of(q * 32, 32), 32), :]
        fhi[2 * w + u], flo[2 * w + u] = halves(f)

    acts = {"as": row_a_start, "a": row_a, "b0": row_b0, "c0": row_c0, "b1": row_b1, "c1": row_c1,
            "root": col_root, "local": col_local, "hop": col_hop, "f": solve}

    def run(where):
        for act in hooks.get(where, ()):
            acts[act[0]](*act[1:])

    run("first")
    for cp in b1:
        cp.wait_recv()
    c1 = send(D.at[1, :, c], D.at[1, :, c], s3s.at[1], s3r.at[1], at(0, 0, 0, 1))
    c1.start()
    for cp in b0:
        cp.wait_recv()
    c0 = send(D.at[0, :, c], D.at[0, :, c], s3s.at[0], s3r.at[0], at(0, 0, 0, 1))
    c0.start()
    own.wait()
    run("second")
    c1.wait_recv()
    c0.wait_recv()
    run("start")
    sub = lax.broadcasted_iota(jnp.int32, (8, 128), 0)
    for g in range(64):
        yy, cc, qq = g // 16, (g // 8) % 2, (2 * g) % 16
        for h in range(2):
            e, o = D[h, yy, cc, qq], D[h, yy, cc, qq + 1]
            M[8 * g:8 * g + 8, 256 * h:256 * h + 128] = jnp.where(sub < 4, e, pltpu.roll(o, 4, 0))
            M[8 * g:8 * g + 8, 256 * h + 128:256 * h + 256] = jnp.where(sub < 4, pltpu.roll(e, 4, 0), o)
    chol_body(M, T, U, run)
    l0[...] = right3(M[:256, :256].T)
    l1[...] = right3(M[256:, :].T)
    lblk[...] = U[:, pl.ds(pl.multiple_of((p // 2) * 128, 128), 128)].T
    run("end")
    col_end()
    for cp in a0 + a1 + b0 + b1 + [c0, c1] + ra + [cp for k in rb for cp in rb[k]] + list(rc.values()):
        cp.wait_send()


CHUNKS = ((0, None), (1, None), (3, None), (2, 0), (2, 1))


def default_hooks():
    return {
        "first": [("as",)],
        "second": [("a",), ("root", 0)],
        "start": [("hop", 0, 1)],
        0: [("b0",), ("root", 1, 2), ("b1",)],
        2: [("hop", 0, 2)],
        4: [("hop", 1, 1)],
        6: [("hop", 2, 1), ("hop", 0, 3)],
        7: [("c0",), ("root", 3, 4), ("local",), ("hop", 1, 2)],
        8: [("hop", 3, 1)],
        9: [("hop", 4, 1), ("hop", 2, 2)],
        11: [("hop", 3, 2), ("hop", 1, 3)],
        12: [("hop", 4, 2)],
        13: [("hop", 2, 3)],
        14: [("hop", 3, 3)],
        "end": [("f", 0, 0), ("f", 1, 0), ("hop", 4, 3), ("c1",), ("f", 0, 1), ("f", 1, 1)],
    }


def gather_factor(d, panel):
    dma = pltpu.SemaphoreType.DMA
    vmem = pl.BlockSpec(memory_space=pltpu.VMEM)
    return pl.pallas_call(
        functools.partial(gather_factor_kernel, default_hooks()),
        out_shape=[jax.ShapeDtypeStruct((128, 512), F32), jax.ShapeDtypeStruct((768, 256), BF16), jax.ShapeDtypeStruct((1536, 256), BF16),
                   jax.ShapeDtypeStruct((4, 512, 512), BF16), jax.ShapeDtypeStruct((4, 512, 512), BF16),
                   jax.ShapeDtypeStruct((4, 32, 512), F32), jax.ShapeDtypeStruct((2, 4, 4, 32, 512), F32)],
        in_specs=[pl.BlockSpec(memory_space=pl.ANY)] * 2,
        out_specs=[vmem] * 7,
        scratch_shapes=[pltpu.VMEM((2, 2, 4, 4, 32, 512), F32), pltpu.VMEM((512, 512), F32), pltpu.VMEM((2, 4, 2, 16, 8, 128), F32), pltpu.VMEM((512, 512), F32), pltpu.VMEM((128, 256), F32),
                        pltpu.VMEM((512, 512), F32), dma((18,)), dma((18,)), dma((18,)), dma((18,)), dma((2,)), dma((2,)),
                        dma((18,)), dma((18,)), dma((2, 5, 2)), dma((2, 5)), dma((4,))],
        compiler_params=pltpu.CompilerParams(collective_id=0, has_side_effects=True, vmem_limit_bytes=24 << 20),
        cost_estimate=pl.CostEstimate(flops=4 * 10**10, bytes_accessed=80 << 20, transcendentals=0),
        name="gather_factor",
    )(d, panel)


def per_device(diag_block, panel, trailing):
    d = diag_block.reshape(4, 4, 128).transpose(1, 0, 2).reshape(2, 8, 128)
    lblk, l0, l1, fhi, flo, fpan, xcol = gather_factor(d, panel.reshape(2, 2, 32, 512))
    c = trailing.reshape(4, 512, 2, 4, 128).transpose(0, 1, 3, 2, 4).reshape(16384, 128)
    factor_diag, factor_panel, out = update(lblk, l0, l1, fhi, flo, fpan, xcol.reshape(1024, 512), c)
    updated = out.reshape(4, 512, 4, 2, 128).transpose(0, 1, 3, 2, 4).reshape(4, 512, 2, 512)
    return factor_diag, factor_panel, updated


def solution(mesh):
    specs = (P(("prow", "pcol"), None), P(None, ("prow", "pcol"), None), P(None, "prow", None, "pcol"))
    return jax.shard_map(per_device, mesh=mesh, in_specs=specs, out_specs=specs, check_vma=False)
```

```python
import functools

import jax
import jax.numpy as jnp
from jax import lax
from jax.experimental import pallas as pl
from jax.experimental.pallas import tpu as pltpu
from jax.sharding import PartitionSpec as P

F32 = jnp.float32
BF16 = jnp.bfloat16
HI = lax.Precision.HIGHEST
MESH = pl.DeviceIdType.MESH


def tdot(a, b, prec=HI):
    return lax.dot_general(a, b, (((0,), (0,)), ((), ())), precision=prec, preferred_element_type=F32)

def bc(col, n=128):
    return jnp.broadcast_to(col, (col.shape[0], n))

def elim8(G, c0, sub):
    n = len(G)
    C = [[bc(G[g][:, c0 + j:c0 + j + 1]) for j in range(8)] for g in range(n)]
    L = [G[g][:, :128] for g in range(n)]
    V = [G[g][:, 128:] for g in range(n)]
    dv = None
    for j in range(8):
        piv = [jnp.broadcast_to(C[0][l][j:j + 1, :], (8, 128)) for l in range(j, 8)]
        rinv = 1.0 / piv[0]
        rowL = jnp.broadcast_to(L[0][j:j + 1, :], (8, 128))
        rowV = jnp.broadcast_to(V[0][j:j + 1, :], (8, 128))
        dv = piv[0] if j == 0 else jnp.where(sub == j, piv[0], dv)
        for g in range(n):
            m = C[g][j] * rinv
            if g == 0:
                m = jnp.where(sub > j, m, 0.0)
            for l in range(j + 1, 8):
                C[g][l] = C[g][l] - m * piv[l - j]
            L[g] = L[g] - m * rowL
            V[g] = V[g] - m * rowV
    sc = lax.rsqrt(dv)
    L[0] = L[0] * sc
    V[0] = V[0] * sc
    return [jnp.concatenate([L[g], V[g]], 1) for g in range(n)]

def leaf(T, hook, k):
    sub = lax.broadcasted_iota(jnp.int32, (8, 128), 0)
    for sb in range(4):
        r0 = 32 * sb
        G = [T[r0 + 8 * g:r0 + 8 * g + 8, :] for g in range(4)]
        done = []
        for g in range(4):
            G = elim8(G, r0 + 8 * g, sub)
            done.append(G[0])
            T[r0 + 8 * g:r0 + 8 * g + 8, :] = G[0]
            G = G[1:]
        hook(4 * k + sb)
        if sb < 3:
            W = jnp.concatenate(done, 0)
            Pm = tdot(W[:, :128], W)
            T[r0 + 32:128, :] = T[r0 + 32:128, :] - Pm[r0 + 32:128, :]

def chol_body(M, T, U, hook, nb=4):
    row = lax.broadcasted_iota(jnp.int32, (128, 128), 0)
    col = lax.broadcasted_iota(jnp.int32, (128, 128), 1)
    eye = jnp.where(row == col, 1.0, 0.0).astype(F32)
    n = nb * 128
    for k in range(nb):
        a, b = k * 128, (k + 1) * 128
        T[:, :128] = M[a:b, a:b]
        T[:, 128:] = eye
        leaf(T, hook, k)
        Ukk = jnp.where(col >= row, T[:, :128], 0.0)
        Vkk = jnp.where(col <= row, T[:, 128:], 0.0)
        U[a:b, a:b] = Ukk
        if k > 0:
            U[a:b, :a] = jnp.zeros((128, a), F32)
            M[a:b, :a] = jnp.dot(Vkk, M[a:b, :a], precision=HI, preferred_element_type=F32)
        M[a:b, a:b] = Vkk
        if k < nb - 1:
            Ur = jnp.dot(Vkk, M[a:b, b:], precision=HI, preferred_element_type=F32)
            U[a:b, b:] = Ur
            M[a:b, b:] = jnp.zeros((128, n - b), F32)
            if k > 0:
                M[b:, :a] = M[b:, :a] - tdot(Ur, M[a:b, :a])
            M[b:, a:b] = -tdot(Ur, Vkk)
            M[b:, b:] = M[b:, b:] - tdot(Ur, Ur)


def halves(x):
    hi = x.astype(BF16)
    return hi, (x - hi.astype(F32)).astype(BF16)


def left3(x):
    hi, lo = halves(x)
    return jnp.concatenate([hi, hi, lo], 1)


def right3(x):
    hi, lo = halves(x)
    return jnp.concatenate([hi, lo, hi], 0)


def bdot(a, b):
    return jnp.dot(a, b, preferred_element_type=F32)


def solve_rows(x, l0, l1):
    return jnp.concatenate([bdot(left3(x[:, :256]), l0), bdot(left3(x), l1)], 1)


ROWS = 128


def update_kernel(lblk, l0, l1, fhi, flo, frows, xcol, c, fdiag, fpan, out, cols, made, sems):
    p, q = lax.axis_index("prow"), lax.axis_index("pcol")
    pair = lblk[pl.ds(pl.multiple_of((p % 2) * 64 + (q // 2) * 8, 8), 8), :]
    fdiag[...] = jnp.where(q % 2 == 0, pair[:4], pair[4:])
    fpan[...] = frows[...]
    for k in range(4):
        f = solve_rows(xcol[256 * k:256 * (k + 1), :], l0[...], l1[...])
        cols[:, 256 * k:256 * (k + 1)] = right3(f.T)

    copies = []
    for u in range(4):
        f3 = jnp.concatenate([fhi[u], fhi[u], flo[u]], 1)

        def product(v, r):
            prod = bdot(f3[r:r + ROWS], cols[:, 512 * v:512 * (v + 1)])
            for t in range(4):
                at = pl.ds(8 * (512 * u + r) + 2 * t + v, ROWS, stride=8)
                made[at, :] = c[at, :] - prod[:, 128 * t:128 * (t + 1)]

        def keep(v, r):
            for t in range(4):
                at = pl.ds(8 * (512 * u + r) + 2 * t + v, ROWS, stride=8)
                made[at, :] = c[at, :]

        def both(v, r):
            present = v * 16 + q <= u * 8 + p
            pl.when(present)(functools.partial(product, v, r))
            pl.when(jnp.logical_not(present))(functools.partial(keep, v, r))

        for r in range(0, 512, ROWS):
            for v in range(2):
                if v == u // 2:
                    both(v, r)
                elif v < u // 2:
                    product(v, r)
                else:
                    keep(v, r)
            at = pl.ds(8 * (512 * u + r), 8 * ROWS)
            cp = pltpu.make_async_copy(made.at[at], out.at[at], sems.at[len(copies)])
            cp.start()
            copies.append(cp)
    for cp in copies:
        cp.wait()


def update(lblk, l0, l1, fhi, flo, frows, xcol, c):
    vmem = pl.BlockSpec(memory_space=pltpu.VMEM)
    return pl.pallas_call(
        update_kernel,
        in_specs=[vmem] * 8,
        out_specs=[vmem, vmem, pl.BlockSpec(memory_space=pltpu.HBM)],
        out_shape=[jax.ShapeDtypeStruct((4, 512), F32), jax.ShapeDtypeStruct((4, 32, 512), F32),
                   jax.ShapeDtypeStruct((16384, 128), F32)],
        scratch_shapes=[pltpu.VMEM((1536, 1024), BF16), pltpu.VMEM((16384, 128), F32), pltpu.SemaphoreType.DMA((2048 // ROWS,))],
        compiler_params=pltpu.CompilerParams(vmem_limit_bytes=26 << 20),
        name="panel_update",
    )(lblk, l0, l1, fhi, flo, frows, xcol, c)


def gather_factor_kernel(hooks, d, panel, lblk, l0, l1, fhi, flo, fpan, xcol, xrow, fs, D, M, T, U, s1s, s1r, s2s, s2r, s3s, s3r, rs, rr, cs, cr, loc):
    p, q = lax.axis_index("prow"), lax.axis_index("pcol")
    y, c, x, z = p // 2, p % 2, q // 4, q % 4

    def at(dx, dy, dz, dc=0):
        return (lax.rem(y + dy, 4) * 2 + lax.rem(c + dc, 2), lax.rem(x + dx, 4) * 4 + lax.rem(z + dz, 4))

    def send(src, dst, ssem, rsem, dev):
        return pltpu.make_async_remote_copy(src_ref=src, dst_ref=dst, send_sem=ssem, recv_sem=rsem, device_id=dev, device_id_type=MESH)

    plane = [(dx, dz) for dx in range(4) for dz in range(4) if dx or dz]
    barrier = pltpu.get_barrier_semaphore()
    for dev in [at(dx, 0, dz) for dx, dz in plane] + [at(0, dy, 0) for dy in (1, 2, 3)] + [at(0, 0, 0, 1)]:
        pl.semaphore_signal(barrier, inc=1, device_id=dev, device_id_type=MESH)
    pl.semaphore_wait(barrier, 19)

    a0 = [send(d.at[0], D.at[0, y, c, q], s1s.at[k], s1r.at[k], at(dx, 0, dz)) for k, (dx, dz) in enumerate(plane)]
    a1 = [send(d.at[1], D.at[1, y, c, q], s1s.at[14 + dy], s1r.at[14 + dy], at(0, dy, 0)) for dy in (1, 2, 3)]
    for cp in a1 + a0:
        cp.start()
    dloc = pltpu.make_async_copy(d, D.at[:, y, c, q], loc.at[3])
    dloc.start()
    own = pltpu.make_async_copy(panel, xrow.at[:, :, x, z], loc.at[0])
    own.start()
    for cp in a1:
        cp.wait_recv()
    dloc.wait()
    b1 = [send(D.at[1, :, c, q], D.at[1, :, c, q], s2s.at[k], s2r.at[k], at(dx, 0, dz)) for k, (dx, dz) in enumerate(plane)]
    for cp in b1:
        cp.start()
    for cp in a0:
        cp.wait_recv()
    b0 = [send(D.at[0, y, c], D.at[0, y, c], s2s.at[14 + dy], s2r.at[14 + dy], at(0, dy, 0)) for dy in (1, 2, 3)]
    for cp in b0:
        cp.start()

    first = x // 2

    def place(w):
        return x if w == 0 else z

    def prior(w, n):
        there = lax.rem(place(w) + n, 4) // 2
        return there if w == 0 else lax.rem(first + there + lax.rem(p, 4) // 2, 2)

    def near(w, n):
        return at(0, 0, n) if w == 0 else at(n, 0, 0)

    def line(ref, w, off):
        if w == 0:
            return ref.at[lax.rem(x + off, 4)]
        return ref.at[:, lax.rem(z + off, 4)]

    ra = [send(panel.at[w], xrow.at[w, :, x, z], rs.at[3 * w + n - 1], rr.at[3 * w + n - 1], near(w, n)) for n in (1, 3, 2) for w in (0, 1)]

    def pick(w, n, k):
        u = prior(w, n)
        return xrow.at[w, u if k == 0 else 1 - u]

    def along(w, n):
        return at(n, 0, 0) if w == 0 else at(0, 0, n)

    rb, rc = {}, {}
    for w in (0, 1):
        mate, away = 1 + 2 * lax.rem(place(w), 2), 3 - 2 * lax.rem(place(w), 2)
        for k in (0, 1):
            j = 6 + 3 * (2 * w + k)
            rb[w, k] = []
            for s, n in enumerate((1, 3)):
                ref = line(pick(w, n, k), w, 0)
                rb[w, k].append(send(ref, ref, rs.at[j + s], rr.at[j + s], along(w, n)))
            ref = line(pick(w, 0, 0), w, away if k == 0 else mate)
            rc[w, k] = send(ref, ref, rs.at[j + 2], rr.at[j + 2], along(w, mate if k == 0 else away))

    lag = lax.rem(y - lax.rem(q, 8) // 2 + 4, 4)
    same = c == lax.rem(q, 2)
    is_root = p == lax.rem(q, 8)

    def chunk(ref, v, i):
        off, part = CHUNKS[i]
        ref = line(ref, v, off)
        return ref if part is None else ref.at[pl.ds(2 * part, 2)]

    def chain(src, v, i):
        part, spot = chunk(src, v, i), chunk(xcol.at[v], v, i)
        return (send(part, spot, cs.at[v, i, 0], cr.at[v, i], at(0, 1 if v == 0 else 3, 0)),
                send(part, spot, cs.at[v, i, 1], cr.at[v, i], at(0, 0, 0, 1)))

    def hop_of(v):
        return lag if v == 0 else lax.rem(4 - lag, 4)

    def col_root(*chunks):
        @pl.when(is_root)
        def _():
            both = [chain(xrow.at[v, first], v, i) for i in chunks for v in range(2)]
            for nxt, other in both:
                nxt.start()
            for nxt, other in both:
                other.start()

    def col_local():
        @pl.when(is_root)
        def _():
            for v in range(2):
                pltpu.make_async_copy(xrow.at[v, first], xcol.at[v], loc.at[1 + v]).start()

    def col_hop(i, hop):
        for v in range(2):
            @pl.when(jnp.logical_and(same, hop_of(v) == hop))
            def _():
                nxt, other = chain(xcol.at[v], v, i)
                other.wait_recv()
                if hop < 3:
                    nxt.start()
                other.start()

    def col_end():
        for v in range(2):
            for i in range(len(CHUNKS)):
                nxt, other = chain(xcol.at[v], v, i)
                pl.when(jnp.logical_not(same))(other.wait_recv)
                pl.when(same)(other.wait_send)
                pl.when(jnp.logical_and(same, hop_of(v) < 3))(nxt.wait_send)

            @pl.when(is_root)
            def _():
                pltpu.make_async_copy(xrow.at[v, first], xcol.at[v], loc.at[1 + v]).wait()

    def row_a_start():
        for cp in ra:
            cp.start()

    def row_a():
        for cp in ra:
            cp.wait_recv()
        for w in (0, 1):
            for cp in rb[w, 0]:
                cp.start()

    def row_b0():
        for w in (0, 1):
            for cp in rb[w, 0]:
                cp.wait_recv()
            rc[w, 0].start()

    def row_b1():
        for w in (0, 1):
            rc[w, 1].start()
            for cp in rb[w, 1]:
                cp.start()

    def row_c0():
        for w in (0, 1):
            rc[w, 0].wait_recv()

    def row_c1():
        for w in (0, 1):
            for cp in rb[w, 1] + [rc[w, 1]]:
                cp.wait_recv()

    def solve(w, k):
        u = prior(w, 0) if k == 0 else 1 - prior(w, 0)
        f = solve_rows(xrow[w, u].reshape(512, 512), l0[...], l1[...])
        fs[...] = f
        fpan[2 * w + u] = fs[pl.ds(pl.multiple_of(q * 32, 32), 32), :]
        fhi[2 * w + u], flo[2 * w + u] = halves(f)

    acts = {"as": row_a_start, "a": row_a, "b0": row_b0, "c0": row_c0, "b1": row_b1, "c1": row_c1,
            "root": col_root, "local": col_local, "hop": col_hop, "f": solve}

    def run(where):
        for act in hooks.get(where, ()):
            acts[act[0]](*act[1:])

    run("first")
    for cp in b1:
        cp.wait_recv()
    c1 = send(D.at[1, :, c], D.at[1, :, c], s3s.at[1], s3r.at[1], at(0, 0, 0, 1))
    c1.start()
    for cp in b0:
        cp.wait_recv()
    c0 = send(D.at[0, :, c], D.at[0, :, c], s3s.at[0], s3r.at[0], at(0, 0, 0, 1))
    c0.start()
    own.wait()
    run("second")
    c1.wait_recv()
    c0.wait_recv()
    run("start")
    sub = lax.broadcasted_iota(jnp.int32, (8, 128), 0)
    for g in range(64):
        yy, cc, qq = g // 16, (g // 8) % 2, (2 * g) % 16
        for h in range(2):
            e, o = D[h, yy, cc, qq], D[h, yy, cc, qq + 1]
            M[8 * g:8 * g + 8, 256 * h:256 * h + 128] = jnp.where(sub < 4, e, pltpu.roll(o, 4, 0))
            M[8 * g:8 * g + 8, 256 * h + 128:256 * h + 256] = jnp.where(sub < 4, pltpu.roll(e, 4, 0), o)
    chol_body(M, T, U, run)
    l0[...] = right3(M[:256, :256].T)
    l1[...] = right3(M[256:, :].T)
    lblk[...] = U[:, pl.ds(pl.multiple_of((p // 2) * 128, 128), 128)].T
    run("end")
    col_end()
    for cp in a0 + a1 + b0 + b1 + [c0, c1] + ra + [cp for k in rb for cp in rb[k]] + list(rc.values()):
        cp.wait_send()


CHUNKS = ((0, None), (1, None), (3, None), (2, 0), (2, 1))


def default_hooks():
    return {
        "first": [("as",)],
        "second": [("a",), ("root", 0)],
        "start": [("hop", 0, 1)],
        0: [("b0",), ("root", 1, 2), ("b1",)],
        2: [("hop", 0, 2)],
        4: [("hop", 1, 1)],
        6: [("hop", 2, 1), ("hop", 0, 3)],
        7: [("c0",), ("root", 3, 4), ("local",), ("hop", 1, 2)],
        8: [("hop", 3, 1)],
        9: [("hop", 4, 1), ("hop", 2, 2)],
        11: [("hop", 3, 2), ("hop", 1, 3)],
        12: [("hop", 4, 2)],
        13: [("hop", 2, 3)],
        14: [("hop", 3, 3)],
        "end": [("f", 0, 0), ("f", 1, 0), ("hop", 4, 3), ("c1",), ("f", 0, 1), ("f", 1, 1)],
    }


def gather_factor(d, panel):
    dma = pltpu.SemaphoreType.DMA
    vmem = pl.BlockSpec(memory_space=pltpu.VMEM)
    return pl.pallas_call(
        functools.partial(gather_factor_kernel, default_hooks()),
        out_shape=[jax.ShapeDtypeStruct((128, 512), F32), jax.ShapeDtypeStruct((768, 256), BF16), jax.ShapeDtypeStruct((1536, 256), BF16),
                   jax.ShapeDtypeStruct((4, 512, 512), BF16), jax.ShapeDtypeStruct((4, 512, 512), BF16),
                   jax.ShapeDtypeStruct((4, 32, 512), F32), jax.ShapeDtypeStruct((2, 4, 4, 32, 512), F32)],
        in_specs=[pl.BlockSpec(memory_space=pl.ANY)] * 2,
        out_specs=[vmem] * 7,
        scratch_shapes=[pltpu.VMEM((2, 2, 4, 4, 32, 512), F32), pltpu.VMEM((512, 512), F32), pltpu.VMEM((2, 4, 2, 16, 8, 128), F32), pltpu.VMEM((512, 512), F32), pltpu.VMEM((128, 256), F32),
                        pltpu.VMEM((512, 512), F32), dma((18,)), dma((18,)), dma((18,)), dma((18,)), dma((2,)), dma((2,)),
                        dma((18,)), dma((18,)), dma((2, 5, 2)), dma((2, 5)), dma((4,))],
        compiler_params=pltpu.CompilerParams(collective_id=0, has_side_effects=True, vmem_limit_bytes=24 << 20),
        cost_estimate=pl.CostEstimate(flops=4 * 10**10, bytes_accessed=80 << 20, transcendentals=0),
        name="gather_factor",
    )(d, panel)


def per_device(diag_block, panel, trailing):
    d = diag_block.reshape(4, 4, 128).transpose(1, 0, 2).reshape(2, 8, 128)
    lblk, l0, l1, fhi, flo, fpan, xcol = gather_factor(d, panel.reshape(2, 2, 32, 512))
    c = trailing.reshape(4, 512, 2, 4, 128).transpose(0, 1, 3, 2, 4).reshape(16384, 128)
    factor_diag, factor_panel, out = update(lblk, l0, l1, fhi, flo, fpan, xcol.reshape(1024, 512), c)
    updated = out.reshape(4, 512, 4, 2, 128).transpose(0, 1, 3, 2, 4).reshape(4, 512, 2, 512)
    return factor_diag, factor_panel, updated


def solution(mesh):
    specs = (P(("prow", "pcol"), None), P(None, ("prow", "pcol"), None), P(None, "prow", None, "pcol"))
    return jax.shard_map(per_device, mesh=mesh, in_specs=specs, out_specs=specs, check_vma=False)
```
